128 devices in a mesh: owner: 16 (over x, y), tensor: 8 (over z, core).
Axes of the slice: x: 4, y: 4, z: 4, core: 2. Of those that a mesh axis runs over, the one named last changes fastest.
Arguments:
- act_rows: bfloat16 [4096, 8192], P('owner', 'tensor'), may hold values from -6 to 6
- base_weight: bfloat16 [8192, 28672], P('tensor', 'owner'), may hold values from -0.0625 to 0.0625
- factor_down: bfloat16 [128, 64, 8192], P('owner', None, 'tensor'), may hold values from -0.0625 to 0.0625
- factor_up: bfloat16 [128, 64, 28672], P(None, None, ('owner', 'tensor')), may hold values from -0.75 to 0.75
- block_adapter: int32 [32], replicated, may hold values from 0 to 127
Outputs:
- projected: bfloat16 [4096, 28672], P('tensor', 'owner')
The draws below stay inside these ranges and needn't reach their ends.
Inputs may be any that keep to these rules, and one draw needn't show every extreme that they name: `block_adapter`: block b holds rows b * 128 to (b + 1) * 128 - 1; each block uses one adapter; one adapter may serve several blocks, not necessarily adjacent ones.
All inputs are finite; a program needn't handle non-finite values.
Results may differ from the reference program's by a relative error of at most 0.018.
Values may be sent and summed in bfloat16 or wider, within the bound.
No kernel may reach another device: no remote copies, remote signals or barrier semaphores. Data moves between devices by JAX's collectives and lax.ppermute only.
A program may use at most 128 MiB of HBM per device.

```python
import math
import jax
import jax.numpy as jnp
import numpy as np
from jax import lax

D = 8192
F = 28672
R = 64
ADAPTERS = 128
BLK = 128
TOKEN_ROWS_TOTAL = 4096
NBLK = 32
N_OWNER = 16
N_TENSOR = 8


def plant(result, key, least, largest):
    spot = [jax.random.randint(jax.random.fold_in(key, axis), (), 0, length) for axis, length in enumerate(result.shape)]
    main_axis = result.shape.index(max(result.shape))
    neighbour = spot[:main_axis] + [(spot[main_axis] + 1) % result.shape[main_axis]] + spot[main_axis + 1:]
    return result.at[tuple(spot)].set(least).at[tuple(neighbour)].set(largest)


def shard_levels(rng, shape, shards, least, high):
    level = 1.0
    for position, shards_of in shards:
        steps = jax.random.uniform(jax.random.fold_in(jax.random.fold_in(rng, 6), position), (shards_of,), jnp.float32, least / len(shards), high / len(shards))
        level = level * jnp.repeat(jnp.exp(steps), shape[position] // shards_of).reshape((-1,) + (1,) * (len(shape) - 1 - position))
    return level


def cumulative_ranks(number_of, lean):
    loads = [(1 << 20) // math.isqrt(standing ** lean) + 1 for standing in range(1, number_of + 1)]
    deviation = 1 + sum(loads) // (1 << 30)
    return np.cumsum(np.array([max(1, weight // deviation) for weight in loads]))


def ranked_ids(rng, shape, number_of, lean):
    listing = cumulative_ranks(number_of, lean)
    lot = jax.random.randint(jax.random.fold_in(rng, 1), shape, 0, int(listing[number_of - 1]))
    rank = jnp.searchsorted(jnp.asarray(listing, jnp.int32), lot, side="right")
    return jax.random.permutation(jax.random.fold_in(rng, 2), number_of)[rank].astype(jnp.int32)


def scatter_about(rng, dims, deviation, limit, cuts=(), kind=jnp.bfloat16):
    factor_of = shard_levels(rng, dims, cuts, -0.22, 0.18) if cuts else 1.0
    result = jax.random.normal(rng, dims, jnp.float32) * deviation * factor_of
    return jnp.minimum(jnp.maximum(result, -limit), limit).astype(kind)


def setup_inputs(seed: int = 0) -> dict:
    keys = jax.random.split(jax.random.key(seed), 6)
    return {
        "act_rows": scatter_about(keys[0], (TOKEN_ROWS_TOTAL, D), 1.0, 6.0, ((0, 16), (1, 8))),
        "base_weight": scatter_about(keys[1], (D, F), D ** -0.5, 0.0625, ((0, 8), (1, 16))),
        "factor_down": scatter_about(keys[2], (ADAPTERS, R, D), D ** -0.5, 0.0625, ((0, 16), (2, 8))),
        "factor_up": scatter_about(keys[3], (ADAPTERS, R, F), R ** -0.5, 0.75, ((2, 128),)),
        "block_adapter": plant(ranked_ids(keys[4], (NBLK,), ADAPTERS, 2), jax.random.fold_in(keys[4], 3), 0, ADAPTERS - 1).astype(jnp.int32),
    }


def reference(act_rows, base_weight, factor_down, factor_up, block_adapter):
    slice_width = D // N_TENSOR
    col_width = F // (N_OWNER * N_TENSOR)
    segment_grouped = act_rows.reshape(NBLK, BLK, D)

    def one_block(inputs):
        block_rows, adapter_id = inputs
        down_tile = lax.dynamic_index_in_dim(factor_down, adapter_id.astype(jnp.int32), 0, keepdims=False)
        shrink = jnp.dot(block_rows, down_tile.T, preferred_element_type=jnp.float32).astype(jnp.bfloat16)
        up_tile = lax.dynamic_index_in_dim(factor_up, adapter_id.astype(jnp.int32), 0, keepdims=False)
        return jnp.dot(shrink, up_tile, preferred_element_type=jnp.float32).astype(jnp.bfloat16)

    adapter_term = lax.map(one_block, (segment_grouped, block_adapter)).reshape(TOKEN_ROWS_TOTAL, F)
    col_block = (jnp.arange(F, dtype=jnp.int32) // col_width) % N_TENSOR
    base_sum = jnp.zeros((TOKEN_ROWS_TOTAL, F), jnp.float32)
    for weight_tensor_index in range(N_TENSOR):
        begin_col = weight_tensor_index * slice_width
        piece_out = jnp.dot(act_rows[:, begin_col:begin_col + slice_width], base_weight[begin_col:begin_col + slice_width, :], preferred_element_type=jnp.float32)
        selected = (col_block == weight_tensor_index)[None, :]
        piece_out = piece_out + jnp.where(selected, adapter_term.astype(jnp.float32), jnp.float32(0.0))
        rounded_length = lax.optimization_barrier(piece_out.astype(jnp.bfloat16))
        base_sum = base_sum + rounded_length.astype(jnp.float32)
    return base_sum.astype(jnp.bfloat16)
```

```python
import functools

import jax
import jax.numpy as jnp
from jax import lax
from jax.experimental import pallas as pl
from jax.experimental.pallas import tpu as pltpu
from jax.sharding import Mesh, PartitionSpec as P


BF = jnp.bfloat16
F32 = jnp.float32
SMEM = pl.BlockSpec(memory_space=pltpu.SMEM)
VMEM = pl.BlockSpec(memory_space=pltpu.VMEM)
MIB = 1 << 20


def after(v, *deps):
    return lax.optimization_barrier((v, deps))[0]


def take(v, axis, step):
    return lax.ppermute(v, axis, [((i + step) % 4, i) for i in range(4)])


def swap(v):
    return lax.ppermute(v, "c", [(0, 1), (1, 0)])


def sds(*shape):
    return jax.ShapeDtypeStruct(shape, BF)


def call(kernel, name, outs, ins, scratch=(), limit=24, **kw):
    one = not isinstance(outs, (list, tuple))
    res = pl.pallas_call(
        kernel,
        out_shape=outs,
        in_specs=[SMEM if v.dtype == jnp.int32 else VMEM for v in ins],
        out_specs=VMEM if one else [VMEM] * len(outs),
        scratch_shapes=list(scratch),
        compiler_params=pltpu.CompilerParams(vmem_limit_bytes=limit * MIB),
        name=name,
        **kw,
    )(*ins)
    return res


def product_kernel(targets, na, nb, pos, *refs):
    a, b = refs[:na], refs[na:na + nb]
    w0, w1 = refs[na + nb:na + nb + 2]
    outs, xs = refs[na + nb + 2:-1], refs[-1]
    half, cols = w0.shape
    rows = xs.shape[0] // len(targets)
    for i, j in enumerate(targets):
        d = lax.rem(j + 4 - pos[0], 4)
        at = i * rows
        for src in a:
            n = src.shape[1]
            xs[pl.ds(at, n)] = src[d]
            at += n
        for k, src in enumerate(b):
            @pl.when(d == k)
            def _():
                n = src.shape[1]
                for q in range(4):
                    xs[pl.ds(at + q * n, n)] = src[q]
    step = 256
    for s in range(0, cols, step):
        v = jnp.dot(xs[:, :half], w0[:, s:s + step], preferred_element_type=F32)
        v += jnp.dot(xs[:, half:], w1[:, s:s + step], preferred_element_type=F32)
        v = v.astype(BF)
        o = 0
        for i, j in enumerate(targets):
            part = v[i * rows:(i + 1) * rows]
            if j == 2:
                outs[o][:, s:s + step] = part[:rows // 2]
                outs[o + 1][:, s:s + step] = part[rows // 2:]
                o += 2
            else:
                outs[o][:, s:s + step] = part
                o += 1


def product(pos, targets, a, b, w0, w1):
    rows = sum(v.shape[1] for v in a) + (4 * b[0].shape[1] if b else 0)
    half, cols = w0.shape
    outs = []
    for j in targets:
        outs += [sds(rows // 2, cols)] * 2 if j == 2 else [sds(rows, cols)]
    return call(
        functools.partial(product_kernel, targets, len(a), len(b)), "product",
        outs, [pos, *a, *b, w0, w1],
        [pltpu.VMEM((rows * len(targets), 2 * half), BF)], 40)


def join_kernel(lo, hi, p1, p3, q1, q3):
    h = lo.shape[0]
    q1[:h] = (p1[:h].astype(F32) + lo[...].astype(F32)).astype(BF)
    q1[h:] = p1[h:]
    q3[:h] = p3[:h]
    q3[h:] = (p3[h:].astype(F32) + hi[...].astype(F32)).astype(BF)


def join(lo, hi, p1, p3):
    return call(join_kernel, "join", [sds(*p1.shape)] * 2, [lo, hi, p1, p3])


def shrink_kernel(parts, pos, *refs):
    a = [refs[p * 4:p * 4 + 4] for p in range(parts)]
    b = [refs[4 * parts + p * 4:4 * parts + p * 4 + 4] for p in range(parts)]
    f0, f1, out, xs = refs[8 * parts:]
    n = xs.shape[0] // (2 * parts)
    half = f0.shape[2]
    dims = (((1,), (1,)), ((), ()))

    def one(i, carry):
        j, d = i // 4, lax.rem(i, 4)
        local = pos[3 + i]
        zt = lax.rem(pos[1] + j, 4)
        yt = lax.rem(pos[2] + d, 4)
        dx = lax.rem(j + 4 - pos[0], 4)

        @pl.when(local < 0)
        def _():
            out[zt, yt] = jnp.zeros(out.shape[2:], out.dtype)

        @pl.when(local >= 0)
        def _():
            for t in range(4):
                @pl.when(d == t)
                def _():
                    for p in range(parts):
                        xs[pl.ds(p * n, n)] = a[p][t][dx]

                @pl.when(dx == t)
                def _():
                    for p in range(parts):
                        xs[pl.ds((parts + p) * n, n)] = b[p][t][d]
            v = lax.dot_general(xs[:, :half], f0[local], dims, preferred_element_type=F32)
            v += lax.dot_general(xs[:, half:], f1[local], dims, preferred_element_type=F32)
            out[zt, yt] = v.astype(out.dtype)
        return carry

    lax.fori_loop(0, 16, one, 0)


def shrink_of(pos, a, b, f0, f1):
    parts = len(a)
    n, k = a[0][0].shape[1:]
    flat = [v for p in a for v in p] + [v for p in b for v in p]
    return call(
        functools.partial(shrink_kernel, parts), "shrink",
        sds(4, 4, 2 * parts * n, f0.shape[1]), [pos, *flat, f0, f1],
        [pltpu.VMEM((2 * parts * n, k), BF)])


def close_kernel(parts, slot, pos, *refs):
    groups = [refs[3 * g:3 * g + 3] for g in range(parts + 1)]
    sh, up, out = refs[3 * parts + 3:]
    h = groups[0][0].shape[0]
    n = h // parts
    for i in range(2):
        yt = pos[1] + i
        d = lax.rem(yt - pos[0] + 4, 4)
        term = jnp.dot(sh[yt], up[yt], preferred_element_type=F32).astype(BF).astype(F32)
        dst = (i,) if slot is None else (i, pos[2])

        def add(group, src, at):
            v = sum(r[pl.ds(src, n)].astype(F32) for r in group)
            out[dst + (pl.ds(at, n),)] = (v + term[at:at + n]).astype(BF)

        for p in range(parts):
            @pl.when(d == 0)
            def _():
                add(groups[0], p * n, p * n)

            @pl.when(d > 0)
            def _():
                add(groups[1 + p], pl.multiple_of((d + 3) % 4 * n, n), p * n)
            add(groups[1 + p], pl.multiple_of(3 * n + d * n, n), h + p * n)


def close(pos, slot, groups, sh, up):
    shape = (2, sh.shape[1], up.shape[2])
    if slot is not None:
        shape = (2, 2) + shape[1:]
    flat = [v for g in groups for v in g]
    return call(functools.partial(close_kernel, len(groups) - 1, slot), "close",
                sds(*shape), [pos, *flat, sh, up])


def merge_kernel(pos, other, mine, out, sem):
    copies = [pltpu.make_async_copy(other.at[i], out.at[i, pos[2]], sem.at[i]) for i in range(2)]
    for copy in copies:
        copy.start()
    for copy in copies:
        copy.wait()


def merge(pos, other, mine):
    return pl.pallas_call(
        merge_kernel,
        out_shape=sds(*mine.shape),
        in_specs=[SMEM, VMEM, pl.BlockSpec(memory_space=pl.ANY)],
        out_specs=pl.BlockSpec(memory_space=pl.ANY),
        scratch_shapes=[pltpu.SemaphoreType.DMA((2,))],
        input_output_aliases={2: 0},
        name="merge",
    )(pos, other, mine)


def per_device(act, w, down, up, ids):
    x, y, z, c = (lax.axis_index(n) for n in "xyzc")
    ints = lambda *v: jnp.stack(v).astype(jnp.int32)
    half_rows = act.shape[0] // 2
    keep = lax.dynamic_slice_in_dim(act, c * half_rows, half_rows, 0)
    give = lax.dynamic_slice_in_dim(act, (1 - c) * half_rows, half_rows, 0)
    got = swap(give)
    w1 = swap(after(w, got))
    f1 = swap(after(down, got))
    rows = jnp.concatenate([keep, got], 1)
    h = half_rows // 2
    parts = 2
    n = h // parts
    ra, rb = rows[:h], rows[h:]
    pa = [ra] + [take(ra, "x", d) for d in (1, 2, 3)]
    pb = [rb] + [take(rb, "y", d) for d in (1, 2, 3)]
    shift = lax.rem(x - z + 4, 4)
    pos = ints(shift)
    sa = [jnp.stack([v[p * n:(p + 1) * n] for v in pa]) for p in range(parts)]
    sb = [jnp.stack([v[p * n:(p + 1) * n] for v in pb]) for p in range(parts)]

    def spread(p):
        return ([sa[p]] + [take(sa[p], "y", d) for d in (1, 2, 3)],
                [sb[p]] + [take(sb[p], "x", d) for d in (1, 2, 3)])

    a, b = [None] * parts, [None] * parts
    a[0], b[0] = spread(0)
    g0 = product(pos, (2, 1, 3, 0), sa, [], w, w1)

    def first_half(pl_, pr_):
        return take(pl_, "z", -1), take(pr_, "z", 1)

    def second_half(lo, hi, p1, p3, p0):
        q1, q3 = join(lo, hi, p1, p3)
        return (p0, take(q1, "z", -1), take(q3, "z", 1)), q3

    halves = first_half(g0[0], g0[1])
    sa[1], sb[1] = after((sa[1], sb[1]), g0[2])
    a[1], b[1] = spread(1)
    s0, mark = second_half(*halves, *g0[2:])
    groups = [s0]

    def group(p, mark):
        pa_, pb_ = after((a[p][1:], b[p]), mark)
        p2 = product(pos, (2,), pa_, pb_, w, w1)
        lo_hi = first_half(*p2)
        pa_, pb_ = after((pa_, pb_), p2[0])
        rest = product(pos, (1, 3, 0), pa_, pb_, w, w1)
        return lo_hi, rest

    halves, rest = group(0, mark)

    up = after(up, rest[0])
    table = ids.reshape(4, 4, 2)
    by_target = jnp.transpose(table, (0, 2, 1)).reshape(-1)
    chosen = up[by_target]
    chosen = lax.all_to_all(chosen.reshape(8, 4, *up.shape[1:]), ("z", "c"), 0, 0)
    chosen = jnp.transpose(chosen, (1, 2, 0, 3)).reshape(4, up.shape[1], -1)

    s1, mark = second_half(*halves, *rest)
    groups.append(s1)
    halves, rest = group(1, mark)

    zs = (z + jnp.arange(4)) % 4
    ys = (y + jnp.arange(4)) % 4
    mine = table[zs][:, ys][:, :, c].reshape(16) - down.shape[0] * (x * 4 + y)
    mine = jnp.where((mine >= 0) & (mine < down.shape[0]), mine, -1).astype(jnp.int32)
    sh = shrink_of(jnp.concatenate([ints(shift, z, y), mine]), a, b, down, f1)
    sh = lax.all_to_all(sh, "z", 0, 0).astype(F32).sum(0).astype(BF)
    for axis in ("x", "y"):
        sh = lax.all_to_all(jnp.broadcast_to(sh[None], (4,) + sh.shape), axis, 0, 0)
        sh = sh.astype(F32).sum(0).astype(BF)

    s2, mark = second_half(*halves, *rest)
    groups.append(s2)
    other = swap(close(ints(y, 2 - 2 * c), None, groups, sh, chosen))
    mine = close(ints(y, 2 * c, c), 2, groups, sh, chosen)
    out = merge(ints(y, 2 * c, 1 - c), other, mine)
    return out.reshape(-1, out.shape[-1])


def solution(mesh):
    grid = Mesh(mesh.devices.reshape(4, 4, 4, 2), ("x", "y", "z", "c"))
    o, t = ("x", "y"), ("z", "c")
    in_specs = (P(o, t), P(t, o), P(o, None, t), P(None, None, o + t), P())
    return jax.shard_map(
        per_device, mesh=grid, in_specs=in_specs, out_specs=P(t, o), check_vma=False
    )
```
